256 devices in a mesh: blk: 128 (over x, z, y), row: 2 (over core).
Axes of the slice: x: 4, y: 4, z: 8, core: 2. Of those that a mesh axis runs over, the one named last changes fastest.
Arguments:
- diag_block: float32 [1024, 1024], P('row'), as said below
- panel_rows: float32 [2, 4096, 1024], P('row', 'blk'), may hold values from -6 to 6
- row_ids: int32 [32], replicated, may hold values from 0 to 255, as said below
- col_ids: int32 [768], P('blk'), may hold values from -1 to 255, as said below
- block_rows: int32 [768, 8], P('blk'), may hold values from -1 to 255, as said below
- blocks: float32 [768, 8, 256, 256], P('blk', None, 'row'), may hold values from -6 to 6
Outputs:
- factor_rows: float32 [2, 4096, 1024], P('row', 'blk')
- new_blocks: float32 [768, 8, 256, 256], P('blk', None, 'row')
The draws below stay inside these ranges and needn't reach their ends.
Inputs may be any that keep to these rules, and one draw needn't show every extreme that they name: `row_ids`: strictly increasing and distinct; the last is 255. `col_ids`: each of the 256 block columns stands in exactly one slot; an owner's slots s * 6 to s * 6 + 5 hold its columns first, then -1; owners hold 0 to 6 columns, one owner exactly 6. `block_rows`: for a live slot, entry 0 is its own column, live entries rise strictly and are followed only by -1; an empty slot holds -1 only. A column among row_ids stores the block rows of row_ids from itself on, up to 8 of them. `diag_block`: symmetric positive definite.
All inputs are finite; a program needn't handle non-finite values.
Results may differ from the reference program's by a relative error of at most 0.0003.
Values may be sent and summed in bfloat16 or wider, within the bound.
A program may use at most 128 MiB of HBM per device.

```python
import math
import jax
import jax.numpy as jnp
from jax import lax

BLOCK_SIZE = 256
W = 512
MEAN = 2
CS = 6
STORED_BLOCKS = 8
PR = 32
NCOL = 256
SLOT_COUNT = 768
N_BLK = 128


def edge_weights(key, order):
    return jax.random.uniform(key, (order,), jnp.float32, 32.0, 96.0)


def shifted(values, offset, order):
    return jnp.concatenate([jnp.zeros((offset,), jnp.float32), values[:order - offset]])


def kernel_part(key, order):
    key_place, key_scale = jax.random.split(key, 2)
    places = jax.random.uniform(key_place, (order,), jnp.float32, 0.0, 1.0)
    scales = jnp.exp(jax.random.uniform(key_scale, (order,), jnp.float32, math.log(0.7), math.log(1.4)))
    reach = 20.0 / order
    apart = jnp.abs(places[:, None] - places[None, :])
    return 8.0 * scales[:, None] * scales[None, :] * jnp.exp(-apart / reach)


def draw_diag_block(key, part):
    key_horiz, key_vert, right_random_key, key_left, key_ridge = jax.random.split(key, 5)
    order = 2 * W
    span = W // 16
    index = jnp.arange(order)
    column = index % span
    horiz = edge_weights(key_horiz, order) * ((column < span - 1) & (index + 1 < order)).astype(jnp.float32)
    vert = edge_weights(key_vert, order) * (index + span < order).astype(jnp.float32)
    down_right = edge_weights(right_random_key, order) * ((column < span - 1) & (index + span + 1 < order)).astype(jnp.float32)
    down_left = edge_weights(key_left, order) * ((column > 0) & (index + span - 1 < order)).astype(jnp.float32)
    ridge = 64.0 * jnp.exp(jax.random.uniform(key_ridge, (order,), jnp.float32, math.log(0.02), math.log(0.2)))
    total = horiz + shifted(horiz, 1, order)
    total = total + vert + shifted(vert, span, order)
    total = total + down_right + shifted(down_right, span + 1, order)
    total = total + down_left + shifted(down_left, span - 1, order)
    diagonal = total + ridge
    dense_matrix = jnp.diag(diagonal)
    dense_matrix = dense_matrix - jnp.diag(horiz[:order - 1], 1) - jnp.diag(horiz[:order - 1], -1)
    dense_matrix = dense_matrix - jnp.diag(vert[:order - span], span) - jnp.diag(vert[:order - span], -span)
    dense_matrix = dense_matrix - jnp.diag(down_right[:order - span - 1], span + 1) - jnp.diag(down_right[:order - span - 1], -(span + 1))
    dense_matrix = dense_matrix - jnp.diag(down_left[:order - span + 1], span - 1) - jnp.diag(down_left[:order - span + 1], -(span - 1))
    dense_matrix = dense_matrix + kernel_part(jax.random.fold_in(key, 41), order)
    return dense_matrix


def pattern_rows(key):
    shuffled = jax.random.permutation(jax.random.fold_in(key, 11), NCOL - 1)
    leading = jnp.sort(shuffled[:PR - 1]).astype(jnp.int32)
    return jnp.concatenate([leading, jnp.full((1,), NCOL - 1, jnp.int32)]).astype(jnp.int32)


def owner_columns(key):
    shuffle = jax.random.permutation(jax.random.fold_in(key, 23), N_BLK)
    ranks = jnp.arange(N_BLK)
    by_rank = jnp.where(ranks == 0, 3 * MEAN, MEAN)
    by_rank = jnp.where((ranks == 1) | (ranks == 2) | (ranks == 4), 0, by_rank)
    by_rank = jnp.where(ranks == 3, 2 * MEAN, by_rank)
    counts = jnp.zeros((N_BLK,), jnp.int32).at[shuffle].set(by_rank.astype(jnp.int32))
    live = jnp.arange(CS)[None, :] < counts[:, None]
    flat_live = live.reshape(-1).astype(jnp.int32)
    rank_of = jnp.cumsum(flat_live) - 1
    column_order = jax.random.permutation(jax.random.fold_in(key, 29), NCOL)
    picked = column_order[jnp.clip(rank_of, 0, NCOL - 1)]
    return jnp.where(flat_live > 0, picked, -1).astype(jnp.int32)


def draw_row_ids(key, part):
    return pattern_rows(key)


def draw_col_ids(key, part):
    return owner_columns(key)


def draw_block_rows(key, part):
    columns = owner_columns(key)
    rows = pattern_rows(key)
    match_flags = rows[None, :] == columns[:, None]
    inside = jnp.any(match_flags, axis=1)
    position = jnp.sum(jnp.where(match_flags, jnp.arange(PR)[None, :], 0), axis=1)
    follow = position[:, None] + jnp.arange(STORED_BLOCKS)[None, :]
    set_rows = jnp.where(follow < PR, rows[jnp.clip(follow, 0, PR - 1)], -1)
    stride_steps = jax.random.randint(jax.random.fold_in(key, 31), (SLOT_COUNT, STORED_BLOCKS), 1, 4)
    stride_steps = jnp.where(jnp.arange(STORED_BLOCKS)[None, :] == 0, 0, stride_steps)
    offsets = jnp.cumsum(stride_steps, axis=1)
    loose_rows = columns[:, None] + offsets
    loose_rows = jnp.where(loose_rows < NCOL, loose_rows, -1)
    chosen = jnp.where(inside[:, None], set_rows, loose_rows)
    return jnp.where(columns[:, None] >= 0, chosen, -1).astype(jnp.int32)


def levels(own_key, extent, pieces, low, high):
    gain = 1.0
    for axis_at, blocks in pieces:
        steps = jax.random.uniform(jax.random.fold_in(jax.random.fold_in(own_key, 6), axis_at), (blocks,), jnp.float32, low / len(pieces), high / len(pieces))
        gain = gain * jnp.repeat(jnp.exp(steps), extent[axis_at] // blocks).reshape((-1,) + (1,) * (len(extent) - 1 - axis_at))
    return gain


def centred(own_key, shape, spread, most, cuts=(), held_as=jnp.bfloat16):
    result = spread * jax.random.normal(own_key, shape, jnp.float32)
    if cuts:
        result = result * levels(own_key, shape, cuts, -0.22, 0.18)
    return jnp.clip(result, -most, most).astype(held_as)


def setup_inputs(seed: int = 0) -> dict:
    keys = jax.random.split(jax.random.key(seed), 7)
    return {
        "diag_block": draw_diag_block(jax.random.fold_in(keys[6], 71), 0),
        "panel_rows": centred(keys[1], (2, PR * (BLOCK_SIZE // 2), 2 * W), 1.0, 6.0, ((0, 2), (1, 128)), jnp.float32),
        "row_ids": draw_row_ids(jax.random.fold_in(keys[6], 71), 0),
        "col_ids": draw_col_ids(jax.random.fold_in(keys[6], 71), 0),
        "block_rows": draw_block_rows(jax.random.fold_in(keys[6], 71), 0),
        "blocks": centred(keys[5], (SLOT_COUNT, STORED_BLOCKS, BLOCK_SIZE, BLOCK_SIZE), 1.0, 6.0, ((0, 128), (2, 2)), jnp.float32),
    }


def right_solve(lower_factor, right_side):
    return lax.linalg.triangular_solve(lower_factor, right_side, left_side=False, lower=True, transpose_a=True)

def reference(diag_block, panel_rows, row_ids, col_ids, block_rows, blocks):
    diag_first = diag_block[:W, :W]
    coupling = diag_block[W:, :W]
    diag_second = diag_block[W:, W:]
    factor_first = jnp.linalg.cholesky(diag_first)
    stacked_rows = panel_rows.reshape(2 * PR * (BLOCK_SIZE // 2), 2 * W)
    left_part = right_solve(factor_first, stacked_rows[:, :W])
    coupled = right_solve(factor_first, coupling)
    schur_second = diag_second - jnp.dot(coupled, coupled.T, precision=lax.Precision.HIGHEST)
    factor_second = jnp.linalg.cholesky(schur_second)
    right_rows = stacked_rows[:, W:] - jnp.dot(left_part, coupled.T, precision=lax.Precision.HIGHEST)
    right_part = right_solve(factor_second, right_rows)
    factor_rows = jnp.concatenate([left_part, right_part], axis=1).reshape(2, PR * (BLOCK_SIZE // 2), 2 * W)
    rounded = factor_rows.astype(jnp.bfloat16)
    whole_blocks = rounded.reshape(2, PR, BLOCK_SIZE // 2, 2 * W).transpose(1, 0, 2, 3).reshape(PR, BLOCK_SIZE, 2 * W)
    positions = jnp.arange(PR, dtype=jnp.int32)

    def update(slot_data):
        column, rows_of, stored = slot_data
        col_match = (row_ids == column) & (column >= 0)
        col_index = jnp.sum(jnp.where(col_match, positions, 0)).astype(jnp.int32)
        col_valid = jnp.any(col_match)
        row_match = (row_ids[None, :] == rows_of[:, None]) & (rows_of[:, None] >= 0)
        row_index = jnp.sum(jnp.where(row_match, positions[None, :], 0), axis=1).astype(jnp.int32)
        row_valid = jnp.any(row_match, axis=1) & col_valid
        col_factor = whole_blocks[col_index].astype(jnp.float32)
        row_factor = whole_blocks[row_index].astype(jnp.float32)
        product = jnp.einsum('rab,jb->raj', row_factor, col_factor)
        return stored - jnp.where(row_valid[:, None, None], product, jnp.float32(0.0))
    new_blocks = lax.map(update, (col_ids, block_rows, blocks))
    return (factor_rows, new_blocks)
```

```python
import functools

import jax
import jax.numpy as jnp
from jax import lax
from jax.experimental import pallas as pl
from jax.experimental.pallas import tpu as pltpu
from jax.sharding import PartitionSpec as P

HIGH = lax.Precision.HIGHEST
NB = 128
F32 = jnp.float32


def lane_spread(x, c):
    return jnp.broadcast_to(x[:, c : c + 1], x.shape)


def row_spread(x, m):
    return jnp.broadcast_to(x[m : m + 1, :], x.shape)


def reciprocal(d):
    r = pl.reciprocal(d, approx=True)
    return r * (2.0 - d * r)


def mm(a, b, ca, cb):
    return lax.dot_general(
        a, b, (((ca,), (cb,)), ((), ())), precision=HIGH, preferred_element_type=F32
    )


def block_inverse(rows):
    sub = lax.broadcasted_iota(jnp.int32, (8, NB), 0)
    lane = lax.broadcasted_iota(jnp.int32, (8, NB), 1)
    n = NB // 8
    a = list(rows)
    e = [jnp.where(lane == sub + 8 * k, 1.0, 0.0).astype(F32) for k in range(n)]
    inverse = [None] * n
    pivot = [lane_spread(a[0], m) for m in range(8)]
    for j in range(n):
        d = list(pivot)
        unit = [jnp.where(sub == m, 1.0, 0.0).astype(F32) for m in range(8)]
        diagonal = jnp.ones((8, NB), F32)
        for i in range(8):
            top = row_spread(d[i], i)
            diagonal = jnp.where(sub == i, top, diagonal)
            if i == 7:
                break
            f = jnp.where(sub > i, d[i] * reciprocal(top), 0.0)
            for m in range(i + 1, 8):
                d[m] = d[m] - f * row_spread(d[i], m)
            for m in range(i + 1):
                unit[m] = unit[m] - f * row_spread(unit[m], i)
        scale = lax.rsqrt(diagonal)
        scale = scale * (1.5 - 0.5 * diagonal * scale * scale)
        w = [unit[m] * scale for m in range(8)]
        u = w[0] * row_spread(a[j], 0)
        v = w[0] * row_spread(e[j], 0)
        for m in range(1, 8):
            u = u + w[m] * row_spread(a[j], m)
            v = v + w[m] * row_spread(e[j], m)
        inverse[j] = v
        if j == n - 1:
            break
        ws = {(i, m): row_spread(w[m], i) for i in range(8) for m in range(i + 1)}
        us = [row_spread(u, i) for i in range(8)]
        vs = [row_spread(v, i) for i in range(8)]
        for k in range(j + 1, n):
            below = [lane_spread(a[k], 8 * j + m) for m in range(8)]
            c = []
            for i in range(8):
                t = below[0] * ws[i, 0]
                for m in range(1, i + 1):
                    t = t + below[m] * ws[i, m]
                c.append(t)
            if k == j + 1:
                pivot = []
                for m in range(8):
                    t = c[0] * row_spread(c[0], m)
                    for i in range(1, 8):
                        t = t + c[i] * row_spread(c[i], m)
                    pivot.append(lane_spread(a[k], 8 * k + m) - t)
            ta, te = c[0] * us[0], c[0] * vs[0]
            for i in range(1, 8):
                ta = ta + c[i] * us[i]
                te = te + c[i] * vs[i]
            a[k] = a[k] - ta
            e[k] = e[k] - te
    return jnp.concatenate(inverse, axis=0)


def factor_kernel(s_ref, r_ref, blocks_ref, x_ref, g_ref, copy_ref, u_ref, t_ref, linv_ref, dg_ref, y_ref, sem):
    steps = s_ref.shape[0] // NB
    copy = pltpu.make_async_copy(blocks_ref, copy_ref, sem)
    copy.start()
    u_ref[...] = jnp.zeros_like(u_ref)
    x_ref[...] = jnp.zeros_like(x_ref)
    linv_ref[...] = jnp.zeros_like(linv_ref)
    t_ref[1] = jnp.zeros(t_ref.shape[1:], F32)
    t_ref[0] = s_ref[0:NB, :]
    dg_ref[...] = s_ref[0:NB, 0:NB]
    y_ref[...] = r_ref[:, 0:NB]

    def step(p, carry):
        cur = lax.rem(p, 2)
        oth = 1 - cur
        here = pl.ds(pl.multiple_of(p * NB, NB), NB)
        before = pl.ds(pl.multiple_of(jnp.maximum(p - 1, 0) * NB, NB), NB)
        after = pl.ds(pl.multiple_of(jnp.minimum(p + 1, steps - 1) * NB, NB), NB)
        u_prev = mm(linv_ref[...], t_ref[oth], 1, 0)
        u_ref[before, :] = u_prev
        t_ref[cur] = t_ref[cur] - mm(u_ref[before, here], u_prev, 0, 0)
        t_next = s_ref[after, :] - mm(u_ref[:, after], u_ref[...], 0, 0)
        y_next = r_ref[:, after] - mm(x_ref[...], u_ref[:, after], 1, 0)
        linv = block_inverse([dg_ref[8 * k : 8 * k + 8, :] for k in range(NB // 8)])
        linv_ref[...] = linv
        t_ref[oth] = t_next
        u_after = mm(linv, t_ref[cur, :, after], 1, 0)
        dg_ref[...] = t_ref[oth, :, after] - mm(u_after, u_after, 0, 0)
        x_here = mm(y_ref[...], linv, 1, 1)
        x_ref[:, here] = x_here
        g_ref[p] = x_here.astype(jnp.bfloat16)
        y_ref[...] = y_next - mm(x_here, u_after, 1, 0)
        return carry

    lax.fori_loop(0, steps, step, 0)
    copy.wait()


def factor(diag, rows, blocks):
    order = diag.shape[0]
    vmem = pl.BlockSpec(memory_space=pltpu.VMEM)
    anywhere = pl.BlockSpec(memory_space=pl.ANY)
    return pl.pallas_call(
        factor_kernel,
        out_shape=(
            jax.ShapeDtypeStruct(rows.shape, F32),
            jax.ShapeDtypeStruct((order // NB, rows.shape[0], NB), jnp.bfloat16),
            jax.ShapeDtypeStruct(blocks.shape, F32),
        ),
        in_specs=[vmem, vmem, anywhere],
        out_specs=[vmem, vmem, anywhere],
        scratch_shapes=[
            pltpu.VMEM((order, order), F32),
            pltpu.VMEM((2, NB, order), F32),
            pltpu.VMEM((NB, NB), F32),
            pltpu.VMEM((NB, NB), F32),
            pltpu.VMEM((rows.shape[0], NB), F32),
            pltpu.SemaphoreType.DMA,
        ],
        compiler_params=pltpu.CompilerParams(vmem_limit_bytes=48 << 20),
    )(diag, rows, blocks)


def update_kernel(col_at, row_at, half, g_ref, blocks_ref, out_ref, col_buf, row_buf, blk_buf, col_sem, row_sem, blk_sem):
    slots, stored = blocks_ref.shape[:2]
    chunks = g_ref.shape[0]
    size = blk_buf.shape[2]
    mine = half[0]
    last = g_ref.shape[2] - 1

    def col_copy(s):
        return pltpu.make_async_copy(g_ref.at[:, :, jnp.maximum(col_at[s], 0)], col_buf.at[s], col_sem.at[s])

    def row_copy(s, r):
        at = jnp.minimum(jnp.maximum(row_at[s, r], 0), last)
        return pltpu.make_async_copy(g_ref.at[:, mine, at], row_buf.at[s, r], row_sem.at[s, r])

    def blk_in(s):
        return pltpu.make_async_copy(blocks_ref.at[s], blk_buf.at[s], blk_sem.at[s])

    def blk_out(s):
        return pltpu.make_async_copy(blk_buf.at[s], out_ref.at[s], blk_sem.at[s])

    for s in range(slots):
        @pl.when(col_at[s] >= 0)
        def _():
            col_copy(s).start()
            for r in range(stored):
                row_copy(s, r).start()
            blk_in(s).start()

    for s in range(slots):
        @pl.when(col_at[s] >= 0)
        def _():
            col_copy(s).wait()
            for r in range(stored):
                row_copy(s, r).wait()
            blk_in(s).wait()

            @pl.loop(0, stored)
            def _(r):
                total = jnp.zeros((size, 2 * size), F32)
                for p in range(0, chunks, 2):
                    left = [row_buf[s, r, p + q].reshape(size, NB) for q in range(2)]
                    right = [col_buf[s, p + q].reshape(2 * size, NB) for q in range(2)]
                    total += lax.dot_general(
                        jnp.concatenate(left, axis=1),
                        jnp.concatenate(right, axis=1),
                        (((1,), (1,)), ((), ())),
                        preferred_element_type=F32,
                    )
                kept = blk_buf[s, r]
                blk_buf[s, r] = jnp.where(row_at[s, r] >= 0, kept - total, kept)

            blk_out(s).start()

    for s in range(slots):
        @pl.when(col_at[s] >= 0)
        def _():
            blk_out(s).wait()


def update(g, blocks, col_at, row_at, half):
    slots, stored, size, width = blocks.shape
    chunks, _, _, parts, rows, _ = g.shape
    smem = pl.BlockSpec(memory_space=pltpu.SMEM)
    anywhere = pl.BlockSpec(memory_space=pl.ANY)
    return pl.pallas_call(
        update_kernel,
        out_shape=jax.ShapeDtypeStruct(blocks.shape, F32),
        in_specs=[smem, smem, smem, anywhere, anywhere],
        out_specs=anywhere,
        scratch_shapes=[
            pltpu.VMEM((slots, chunks, 2, parts, rows, NB), jnp.bfloat16),
            pltpu.VMEM((slots, stored, chunks, parts, rows, NB), jnp.bfloat16),
            pltpu.VMEM((slots, stored, size, width), F32),
            pltpu.SemaphoreType.DMA((slots,)),
            pltpu.SemaphoreType.DMA((slots, stored)),
            pltpu.SemaphoreType.DMA((slots,)),
        ],
        input_output_aliases={4: 0},
        compiler_params=pltpu.CompilerParams(vmem_limit_bytes=40 << 20),
    )(col_at, row_at, half, g, blocks)


def places(ids, row_ids):
    match = (row_ids == ids[..., None]) & (ids[..., None] >= 0)
    at = jnp.arange(row_ids.shape[0], dtype=jnp.int32)
    return jnp.max(jnp.where(match, at, -1), axis=-1)


def local(diag_block, panel_rows, row_ids, col_ids, block_rows, blocks):
    pieces = row_ids.shape[0]
    diag = lax.all_gather(diag_block, "row", axis=0, tiled=True)
    x, g, kept = factor(diag, panel_rows[0], blocks)
    gathered = lax.all_gather(g, ("blk", "row"), axis=0, tiled=False)
    chunks, rows = g.shape[:2]
    gathered = gathered.reshape(pieces, -1, 2, chunks, rows, NB).transpose(3, 2, 0, 1, 4, 5)
    col_at = places(col_ids, row_ids)
    row_at = places(block_rows, row_ids)
    half = lax.axis_index("row").astype(jnp.int32)[None]
    return x[None], update(gathered, kept, col_at, row_at, half)


def solution(mesh):
    return jax.shard_map(
        local,
        mesh=mesh,
        in_specs=(
            P("row", None),
            P("row", "blk", None),
            P(),
            P("blk"),
            P("blk", None),
            P("blk", None, "row", None),
        ),
        out_specs=(P("row", "blk", None), P("blk", None, "row", None)),
        check_vma=False,
    )
```

```python
import functools

import jax
import jax.numpy as jnp
from jax import lax
from jax.experimental import pallas as pl
from jax.experimental.pallas import tpu as pltpu
from jax.sharding import PartitionSpec as P

HIGH = lax.Precision.HIGHEST
NB = 128
F32 = jnp.float32
MESH = pl.DeviceIdType.MESH
PLACES = (4, 8, 4)


def lane_spread(x, c):
    return jnp.broadcast_to(x[:, c : c + 1], x.shape)


def row_spread(x, m):
    return jnp.broadcast_to(x[m : m + 1, :], x.shape)


def reciprocal(d):
    r = pl.reciprocal(d, approx=True)
    return r * (2.0 - d * r)


def mm(a, b, ca, cb):
    return lax.dot_general(
        a, b, (((ca,), (cb,)), ((), ())), precision=HIGH, preferred_element_type=F32
    )


def block_inverse(rows):
    sub = lax.broadcasted_iota(jnp.int32, (8, NB), 0)
    lane = lax.broadcasted_iota(jnp.int32, (8, NB), 1)
    n = NB // 8
    a = list(rows)
    e = [jnp.where(lane == sub + 8 * k, 1.0, 0.0).astype(F32) for k in range(n)]
    inverse = [None] * n
    pivot = [lane_spread(a[0], m) for m in range(8)]
    for j in range(n):
        d = list(pivot)
        unit = [jnp.where(sub == m, 1.0, 0.0).astype(F32) for m in range(8)]
        diagonal = jnp.ones((8, NB), F32)
        for i in range(8):
            top = row_spread(d[i], i)
            diagonal = jnp.where(sub == i, top, diagonal)
            if i == 7:
                break
            f = jnp.where(sub > i, d[i] * reciprocal(top), 0.0)
            for m in range(i + 1, 8):
                d[m] = d[m] - f * row_spread(d[i], m)
            for m in range(i + 1):
                unit[m] = unit[m] - f * row_spread(unit[m], i)
        scale = lax.rsqrt(diagonal)
        scale = scale * (1.5 - 0.5 * diagonal * scale * scale)
        w = [unit[m] * scale for m in range(8)]
        u = w[0] * row_spread(a[j], 0)
        v = w[0] * row_spread(e[j], 0)
        for m in range(1, 8):
            u = u + w[m] * row_spread(a[j], m)
            v = v + w[m] * row_spread(e[j], m)
        inverse[j] = v
        if j == n - 1:
            break
        ws = {(i, m): row_spread(w[m], i) for i in range(8) for m in range(i + 1)}
        us = [row_spread(u, i) for i in range(8)]
        vs = [row_spread(v, i) for i in range(8)]
        for k in range(j + 1, n):
            below = [lane_spread(a[k], 8 * j + m) for m in range(8)]
            c = []
            for i in range(8):
                t = below[0] * ws[i, 0]
                for m in range(1, i + 1):
                    t = t + below[m] * ws[i, m]
                c.append(t)
            if k == j + 1:
                pivot = []
                for m in range(8):
                    t = c[0] * row_spread(c[0], m)
                    for i in range(1, 8):
                        t = t + c[i] * row_spread(c[i], m)
                    pivot.append(lane_spread(a[k], 8 * k + m) - t)
            ta, te = c[0] * us[0], c[0] * vs[0]
            for i in range(1, 8):
                ta = ta + c[i] * us[i]
                te = te + c[i] * vs[i]
            a[k] = a[k] - ta
            e[k] = e[k] - te
    return jnp.concatenate(inverse, axis=0)


def spreading(g_ref, own_ref, send_sem, recv_sem, local_sem):
    _, _, nx, nz, ny, rows, _ = g_ref.shape
    blk, h = lax.axis_index("blk"), lax.axis_index("row")
    x, z, y = blk // (nz * ny), (blk // ny) % nz, blk % ny
    first, second = pl.ds(0, rows // 2), pl.ds(rows // 2, rows // 2)
    every = slice(None)

    def device(x, z, y, h):
        return ((x * nz + z) * ny + y, h)

    along_x = [device((x + k) % nx, z, y, h) for k in range(1, nx)]
    along_z = [device(x, (z + k) % nz, y, h) for k in range(1, nz)]
    along_y = [device(x, z, (y + k) % ny, h) for k in range(1, ny)]
    other = device(x, z, y, 1 - h)

    def copies(p, at, pieces):
        return [
            pltpu.make_async_remote_copy(
                src_ref=src,
                dst_ref=dst,
                send_sem=send_sem.at[p, at + i],
                recv_sem=recv_sem.at[p, at + i],
                device_id=target,
                device_id_type=MESH,
            )
            for i, (src, dst, target) in enumerate(pieces)
        ]

    def to_z(p):
        return copies(p, 0, [(own_ref.at[p], g_ref.at[p, h, x, z, y], d) for d in along_z])

    def to_plane(p):
        a, b = g_ref.at[p, h, x, every, y, first], g_ref.at[p, h, x, every, y, second]
        return copies(p, nz - 1, [(a, a, d) for d in along_y] + [(b, b, d) for d in along_x])

    def to_rest(p):
        a, b = g_ref.at[p, h, x, every, every, first], g_ref.at[p, h, every, every, y, second]
        at = nz - 1 + nx - 1 + ny - 1
        return copies(p, at, [(a, a, d) for d in along_x] + [(b, b, d) for d in along_y])

    def to_core(p):
        return copies(p, nz - 1 + 2 * (nx - 1 + ny - 1), [(g_ref.at[p, h], g_ref.at[p, h], other)])

    def keep(p):
        return pltpu.make_async_copy(own_ref.at[p], g_ref.at[p, h, x, z, y], local_sem.at[p])

    return [to_z, to_plane, to_rest, to_core], keep, along_x + along_z + along_y + [other]


def factor_kernel(
    diag_ref, r_ref, x_ref, g_ref,
    s_ref, u_ref, t_ref, linv_ref, dg_ref, y_ref, own_ref,
    strip_send, strip_sem, send_sem, recv_sem, local_sem,
):
    steps = s_ref.shape[0] // NB
    half_steps = steps // 2
    blk, h = lax.axis_index("blk"), lax.axis_index("row")
    stages, keep, peers = spreading(g_ref, own_ref, send_sem, recv_sem, local_sem)

    def strip(i):
        return diag_ref.at[pl.ds(i * NB, NB)], s_ref.at[pl.ds(pl.multiple_of((half_steps * h + i) * NB, NB), NB)]

    def strip_copy(i):
        src, dst = strip(i)
        return pltpu.make_async_copy(src, dst, strip_sem.at[half_steps * h + i])

    def strip_sent(i):
        src, dst = strip(i)
        return pltpu.make_async_remote_copy(
            src_ref=src,
            dst_ref=dst,
            send_sem=strip_send.at[i],
            recv_sem=strip_sem.at[half_steps * h + i],
            device_id=(blk, 1 - h),
            device_id_type=MESH,
        )

    def strip_wait(q):
        dst = s_ref.at[pl.ds(pl.multiple_of(q * NB, NB), NB)]
        pltpu.make_async_copy(diag_ref.at[pl.ds(0, NB)], dst, strip_sem.at[q]).wait()

    def finish(stage, p):
        for copy in stages[stage](p):
            copy.wait_recv()

    def begin(stage, p):
        for copy in stages[stage](p):
            copy.start()

    for i in range(half_steps):
        strip_copy(i).start()
    barrier = pltpu.get_barrier_semaphore()
    for peer in peers:
        pl.semaphore_signal(barrier, inc=1, device_id=peer, device_id_type=MESH)
    u_ref[...] = jnp.zeros_like(u_ref)
    x_ref[...] = jnp.zeros_like(x_ref)
    linv_ref[...] = jnp.zeros_like(linv_ref)
    t_ref[1] = jnp.zeros(t_ref.shape[1:], F32)
    y_ref[...] = r_ref[:, 0:NB]
    pl.semaphore_wait(barrier, len(peers))
    for i in range(half_steps):
        strip_sent(i).start()
    strip_wait(0)
    t_ref[0] = s_ref[0:NB, :]
    dg_ref[...] = s_ref[0:NB, 0:NB]

    def step(p, carry):
        @pl.when(p + 1 < steps)
        def _():
            strip_wait(p + 1)

        @pl.when(p >= 3)
        def _():
            finish(2, p - 3)
            begin(3, p - 3)

        @pl.when(p >= 2)
        def _():
            finish(1, p - 2)
            begin(2, p - 2)

        cur = lax.rem(p, 2)
        oth = 1 - cur
        here = pl.ds(pl.multiple_of(p * NB, NB), NB)
        before = pl.ds(pl.multiple_of(jnp.maximum(p - 1, 0) * NB, NB), NB)
        after = pl.ds(pl.multiple_of(jnp.minimum(p + 1, steps - 1) * NB, NB), NB)
        u_prev = mm(linv_ref[...], t_ref[oth], 1, 0)
        u_ref[before, :] = u_prev
        t_ref[cur] = t_ref[cur] - mm(u_ref[before, here], u_prev, 0, 0)
        t_next = s_ref[after, :] - mm(u_ref[:, after], u_ref[...], 0, 0)
        y_next = r_ref[:, after] - mm(x_ref[...], u_ref[:, after], 1, 0)
        linv = block_inverse([dg_ref[8 * k : 8 * k + 8, :] for k in range(NB // 8)])
        linv_ref[...] = linv
        t_ref[oth] = t_next

        @pl.when(p >= 1)
        def _():
            finish(0, p - 1)
            keep(p - 1).wait()
            begin(1, p - 1)

        x_here = mm(y_ref[...], linv, 1, 1)
        x_ref[:, here] = x_here
        own_ref[p] = x_here.astype(jnp.bfloat16)
        keep(p).start()
        begin(0, p)
        u_after = mm(linv, t_ref[cur, :, after], 1, 0)
        dg_ref[...] = t_ref[oth, :, after] - mm(u_after, u_after, 0, 0)
        y_ref[...] = y_next - mm(x_here, u_after, 1, 0)
        return carry

    lax.fori_loop(0, steps, step, 0)
    last = steps - 1
    finish(2, last - 2)
    begin(3, last - 2)
    finish(1, last - 1)
    begin(2, last - 1)
    finish(0, last)
    keep(last).wait()
    begin(1, last)
    finish(1, last)
    begin(2, last)
    finish(2, last - 1)
    begin(3, last - 1)
    finish(2, last)
    begin(3, last)

    def end(p, carry):
        finish(3, p)
        for stage in stages:
            for copy in stage(p):
                copy.wait_send()
        return carry

    lax.fori_loop(0, steps, end, 0)
    for i in range(half_steps):
        strip_sent(i).wait_send()


def factor(diag, rows, places):
    order = diag.shape[1]
    steps = order // NB
    per = rows.shape[0]
    nx, nz, ny = places
    sends = nz - 1 + 2 * (nx - 1 + ny - 1) + 1
    vmem = pl.BlockSpec(memory_space=pltpu.VMEM)
    anywhere = pl.BlockSpec(memory_space=pl.ANY)
    dma = pltpu.SemaphoreType.DMA
    return pl.pallas_call(
        factor_kernel,
        out_shape=(
            jax.ShapeDtypeStruct(rows.shape, F32),
            jax.ShapeDtypeStruct((steps, 2, nx, nz, ny, per, NB), jnp.bfloat16),
        ),
        in_specs=[anywhere, vmem],
        out_specs=[vmem, anywhere],
        scratch_shapes=[
            pltpu.VMEM((order, order), F32),
            pltpu.VMEM((order, order), F32),
            pltpu.VMEM((2, NB, order), F32),
            pltpu.VMEM((NB, NB), F32),
            pltpu.VMEM((NB, NB), F32),
            pltpu.VMEM((per, NB), F32),
            pltpu.VMEM((steps, per, NB), jnp.bfloat16),
            dma((steps // 2,)),
            dma((steps,)),
            dma((steps, sends)),
            dma((steps, sends)),
            dma((steps,)),
        ],
        compiler_params=pltpu.CompilerParams(
            collective_id=0, has_side_effects=True, vmem_limit_bytes=48 << 20
        ),
    )(diag, rows)


def update_kernel(
    col_at, row_at, half, g_ref, blocks_ref, x_ref, out_ref, x_out,
    col_buf, row_buf, blk_buf, x_buf, col_sem, row_sem, blk_sem, x_sem,
):
    slots, stored = blocks_ref.shape[:2]
    chunks = g_ref.shape[0]
    size = blk_buf.shape[2]
    mine = half[0]
    last = g_ref.shape[2] - 1

    def col_copy(s):
        return pltpu.make_async_copy(g_ref.at[:, :, jnp.maximum(col_at[s], 0)], col_buf.at[s], col_sem.at[s])

    def row_copy(s, r):
        at = jnp.minimum(jnp.maximum(row_at[s, r], 0), last)
        return pltpu.make_async_copy(g_ref.at[:, mine, at], row_buf.at[s, r], row_sem.at[s, r])

    def blk_keep(s):
        return pltpu.make_async_copy(blocks_ref.at[s], out_ref.at[s], blk_sem.at[s])

    def blk_out(s):
        return pltpu.make_async_copy(blk_buf.at[s], out_ref.at[s], blk_sem.at[s])

    x_in = pltpu.make_async_copy(x_ref, x_buf, x_sem.at[0])
    x_back = pltpu.make_async_copy(x_buf, x_out, x_sem.at[1])
    x_in.start()
    for s in range(slots):
        @pl.when(col_at[s] < 0)
        def _():
            blk_keep(s).start()

    for s in range(slots):
        @pl.when(col_at[s] >= 0)
        def _():
            col_copy(s).start()
            for r in range(stored):
                row_copy(s, r).start()

    x_in.wait()
    x_back.start()
    for s in range(slots):
        @pl.when(col_at[s] >= 0)
        def _():
            col_copy(s).wait()
            for r in range(stored):
                row_copy(s, r).wait()

            @pl.loop(0, stored)
            def _(r):
                total = jnp.zeros((size, 2 * size), F32)
                for p in range(0, chunks, 2):
                    left = [row_buf[s, r, p + q].reshape(size, NB) for q in range(2)]
                    right = [col_buf[s, p + q].reshape(2 * size, NB) for q in range(2)]
                    total += lax.dot_general(
                        jnp.concatenate(left, axis=1),
                        jnp.concatenate(right, axis=1),
                        (((1,), (1,)), ((), ())),
                        preferred_element_type=F32,
                    )
                kept = blocks_ref[s, r]
                blk_buf[s, r] = jnp.where(row_at[s, r] >= 0, kept - total, kept)

            blk_out(s).start()

    for s in range(slots):
        @pl.when(col_at[s] >= 0)
        def _():
            blk_out(s).wait()

        @pl.when(col_at[s] < 0)
        def _():
            blk_keep(s).wait()

    x_back.wait()


def update(g, blocks, x, col_at, row_at, half):
    slots, stored, size, width = blocks.shape
    chunks, _, _, parts, rows, _ = g.shape
    smem = pl.BlockSpec(memory_space=pltpu.SMEM)
    anywhere = pl.BlockSpec(memory_space=pl.ANY)
    return pl.pallas_call(
        update_kernel,
        out_shape=(jax.ShapeDtypeStruct(blocks.shape, F32), jax.ShapeDtypeStruct(x.shape, F32)),
        in_specs=[smem, smem, smem, anywhere, pl.BlockSpec(memory_space=pltpu.VMEM), anywhere],
        out_specs=[anywhere, anywhere],
        scratch_shapes=[
            pltpu.VMEM((slots, chunks, 2, parts, rows, NB), jnp.bfloat16),
            pltpu.VMEM((slots, stored, chunks, parts, rows, NB), jnp.bfloat16),
            pltpu.VMEM((slots, stored, size, width), F32),
            pltpu.VMEM(x.shape, F32),
            pltpu.SemaphoreType.DMA((slots,)),
            pltpu.SemaphoreType.DMA((slots, stored)),
            pltpu.SemaphoreType.DMA((slots,)),
            pltpu.SemaphoreType.DMA((2,)),
        ],
        compiler_params=pltpu.CompilerParams(vmem_limit_bytes=50 << 20),
    )(col_at, row_at, half, g, blocks, x)


def places(ids, row_ids):
    match = (row_ids == ids[..., None]) & (ids[..., None] >= 0)
    at = jnp.arange(row_ids.shape[0], dtype=jnp.int32)
    return jnp.max(jnp.where(match, at, -1), axis=-1)


def local(diag_block, panel_rows, row_ids, col_ids, block_rows, blocks):
    pieces = row_ids.shape[0]
    col_at = places(col_ids, row_ids)
    row_at = places(block_rows, row_ids)
    half = lax.axis_index("row").astype(jnp.int32)[None]
    x, g = factor(diag_block, panel_rows[0], PLACES)
    g = g.reshape(g.shape[0], 2, pieces, -1, g.shape[5], NB)
    new_blocks, x = update(g, blocks, x, col_at, row_at, half)
    return x[None], new_blocks


def solution(mesh):
    return jax.shard_map(
        local,
        mesh=mesh,
        in_specs=(
            P("row", None),
            P("row", "blk", None),
            P(),
            P("blk"),
            P("blk", None),
            P("blk", None, "row", None),
        ),
        out_specs=(P("row", "blk", None), P("blk", None, "row", None)),
        check_vma=False,
    )
```

```python
import functools

import jax
import jax.numpy as jnp
from jax import lax
from jax.experimental import pallas as pl
from jax.experimental.pallas import tpu as pltpu
from jax.sharding import PartitionSpec as P

HIGH = lax.Precision.HIGHEST
NB = 128
F32 = jnp.float32
MESH = pl.DeviceIdType.MESH
PLACES = (4, 8, 4)


def lane_spread(x, c):
    return jnp.broadcast_to(x[:, c : c + 1], x.shape)


def row_spread(x, m):
    return jnp.broadcast_to(x[m : m + 1, :], x.shape)


def reciprocal(d):
    r = pl.reciprocal(d, approx=True)
    return r * (2.0 - d * r)


def mm(a, b, ca, cb):
    return lax.dot_general(
        a, b, (((ca,), (cb,)), ((), ())), precision=HIGH, preferred_element_type=F32
    )


def block_inverse(rows):
    sub = lax.broadcasted_iota(jnp.int32, (8, NB), 0)
    lane = lax.broadcasted_iota(jnp.int32, (8, NB), 1)
    n = NB // 8
    a = list(rows)
    e = [jnp.where(lane == sub + 8 * k, 1.0, 0.0).astype(F32) for k in range(n)]
    inverse = [None] * n
    pivot = [lane_spread(a[0], m) for m in range(8)]
    for j in range(n):
        d = list(pivot)
        unit = [jnp.where(sub == m, 1.0, 0.0).astype(F32) for m in range(8)]
        diagonal = jnp.ones((8, NB), F32)
        for i in range(8):
            top = row_spread(d[i], i)
            diagonal = jnp.where(sub == i, top, diagonal)
            if i == 7:
                break
            f = jnp.where(sub > i, d[i] * reciprocal(top), 0.0)
            for m in range(i + 1, 8):
                d[m] = d[m] - f * row_spread(d[i], m)
            for m in range(i + 1):
                unit[m] = unit[m] - f * row_spread(unit[m], i)
        scale = lax.rsqrt(diagonal)
        scale = scale * (1.5 - 0.5 * diagonal * scale * scale)
        w = [unit[m] * scale for m in range(8)]
        u = w[0] * row_spread(a[j], 0)
        v = w[0] * row_spread(e[j], 0)
        for m in range(1, 8):
            u = u + w[m] * row_spread(a[j], m)
            v = v + w[m] * row_spread(e[j], m)
        inverse[j] = v
        if j == n - 1:
            break
        ws = {(i, m): row_spread(w[m], i) for i in range(8) for m in range(i + 1)}
        us = [row_spread(u, i) for i in range(8)]
        vs = [row_spread(v, i) for i in range(8)]
        for k in range(j + 1, n):
            below = [lane_spread(a[k], 8 * j + m) for m in range(8)]
            c = []
            for i in range(8):
                t = below[0] * ws[i, 0]
                for m in range(1, i + 1):
                    t = t + below[m] * ws[i, m]
                c.append(t)
            if k == j + 1:
                pivot = []
                for m in range(8):
                    t = c[0] * row_spread(c[0], m)
                    for i in range(1, 8):
                        t = t + c[i] * row_spread(c[i], m)
                    pivot.append(lane_spread(a[k], 8 * k + m) - t)
            ta, te = c[0] * us[0], c[0] * vs[0]
            for i in range(1, 8):
                ta = ta + c[i] * us[i]
                te = te + c[i] * vs[i]
            a[k] = a[k] - ta
            e[k] = e[k] - te
    return jnp.concatenate(inverse, axis=0)


def spreading(g_ref, own_ref, send_sem, recv_sem, local_sem):
    _, _, nx, nz, ny, rows, _ = g_ref.shape
    blk, h = lax.axis_index("blk"), lax.axis_index("row")
    x, z, y = blk // (nz * ny), (blk // ny) % nz, blk % ny
    first, second = pl.ds(0, rows // 2), pl.ds(rows // 2, rows // 2)
    every = slice(None)

    def device(x, z, y, h):
        return ((x * nz + z) * ny + y, h)

    along_x = [device((x + k) % nx, z, y, h) for k in range(1, nx)]
    along_z = [device(x, (z + k) % nz, y, h) for k in range(1, nz)]
    along_y = [device(x, z, (y + k) % ny, h) for k in range(1, ny)]
    other = device(x, z, y, 1 - h)

    def copies(p, at, pieces):
        return [
            pltpu.make_async_remote_copy(
                src_ref=src,
                dst_ref=dst,
                send_sem=send_sem.at[p, at + i],
                recv_sem=recv_sem.at[p, at + i],
                device_id=target,
                device_id_type=MESH,
            )
            for i, (src, dst, target) in enumerate(pieces)
        ]

    def to_z(p):
        return copies(p, 0, [(own_ref.at[p], g_ref.at[p, h, x, z, y], d) for d in along_z])

    def to_plane(p):
        a, b = g_ref.at[p, h, x, every, y, first], g_ref.at[p, h, x, every, y, second]
        return copies(p, nz - 1, [(a, a, d) for d in along_y] + [(b, b, d) for d in along_x])

    plane = nz - 1 + nx - 1 + ny - 1
    right, left = (x + 1) % nx, (x + nx - 1) % nx
    up, down = (y + 1) % ny, (y + ny - 1) % ny

    def to_next(p):
        a, b = g_ref.at[p, h, x, every, every, first], g_ref.at[p, h, every, every, y, second]
        return copies(p, plane, [
            (a, a, device(right, z, y, h)), (a, a, device(left, z, y, h)),
            (b, b, device(x, z, up, h)), (b, b, device(x, z, down, h)),
        ])

    def to_far(p):
        low, high = pl.ds(0, nz // 2), pl.ds(nz // 2, nz // 2)
        a, b = g_ref.at[p, h, left, low, every, first], g_ref.at[p, h, right, high, every, first]
        c, d = g_ref.at[p, h, every, low, down, second], g_ref.at[p, h, every, high, up, second]
        return copies(p, plane + 4, [
            (a, a, device(right, z, y, h)), (b, b, device(left, z, y, h)),
            (c, c, device(x, z, up, h)), (d, d, device(x, z, down, h)),
        ])

    def to_core(p):
        return copies(p, plane + 8, [(g_ref.at[p, h], g_ref.at[p, h], other)])

    def keep(p):
        return pltpu.make_async_copy(own_ref.at[p], g_ref.at[p, h, x, z, y], local_sem.at[p])

    return [to_z, to_plane, to_next, to_far, to_core], keep, along_x + along_z + along_y + [other]


def factor_kernel(
    diag_ref, r_ref, x_ref, g_ref,
    s_ref, u_ref, t_ref, linv_ref, dg_ref, y_ref, own_ref,
    strip_send, strip_sem, send_sem, recv_sem, local_sem,
):
    steps = s_ref.shape[0] // NB
    half_steps = steps // 2
    blk, h = lax.axis_index("blk"), lax.axis_index("row")
    stages, keep, peers = spreading(g_ref, own_ref, send_sem, recv_sem, local_sem)

    def strip(i):
        return diag_ref.at[pl.ds(i * NB, NB)], s_ref.at[pl.ds(pl.multiple_of((half_steps * h + i) * NB, NB), NB)]

    def strip_copy(i):
        src, dst = strip(i)
        return pltpu.make_async_copy(src, dst, strip_sem.at[half_steps * h + i])

    def strip_sent(i):
        src, dst = strip(i)
        return pltpu.make_async_remote_copy(
            src_ref=src,
            dst_ref=dst,
            send_sem=strip_send.at[i],
            recv_sem=strip_sem.at[half_steps * h + i],
            device_id=(blk, 1 - h),
            device_id_type=MESH,
        )

    def strip_wait(q):
        dst = s_ref.at[pl.ds(pl.multiple_of(q * NB, NB), NB)]
        pltpu.make_async_copy(diag_ref.at[pl.ds(0, NB)], dst, strip_sem.at[q]).wait()

    def finish(stage, p):
        for copy in stages[stage](p):
            copy.wait_recv()

    def begin(stage, p):
        for copy in stages[stage](p):
            copy.start()

    def advance(stage, p):
        finish(stage - 1, p)
        if stage == 1:
            keep(p).wait()
        begin(stage, p)

    for i in range(half_steps):
        strip_copy(i).start()
    barrier = pltpu.get_barrier_semaphore()
    for peer in peers:
        pl.semaphore_signal(barrier, inc=1, device_id=peer, device_id_type=MESH)
    u_ref[...] = jnp.zeros_like(u_ref)
    x_ref[...] = jnp.zeros_like(x_ref)
    linv_ref[...] = jnp.zeros_like(linv_ref)
    t_ref[1] = jnp.zeros(t_ref.shape[1:], F32)
    y_ref[...] = r_ref[:, 0:NB]
    pl.semaphore_wait(barrier, len(peers))
    for i in range(half_steps):
        strip_sent(i).start()
    strip_wait(0)
    t_ref[0] = s_ref[0:NB, :]
    dg_ref[...] = s_ref[0:NB, 0:NB]

    def step(p, carry, begin_at, end_at):
        @pl.when(p + 1 < steps)
        def _():
            strip_wait(p + 1)

        cur = lax.rem(p, 2)
        oth = 1 - cur
        done, todo = slice(0, (end_at - 1) * NB), slice(begin_at * NB, steps * NB)
        here = pl.ds(pl.multiple_of(p * NB, NB), NB)
        before = pl.ds(pl.multiple_of(jnp.maximum(p - 1, 0) * NB, NB), NB)
        after = pl.ds(pl.multiple_of(jnp.minimum(p + 1, steps - 1) * NB, NB), NB)
        u_prev = mm(linv_ref[...], t_ref[oth, :, todo], 1, 0)
        u_ref[before, todo] = u_prev
        t_ref[cur, :, todo] = t_ref[cur, :, todo] - mm(u_ref[before, here], u_prev, 0, 0)
        t_next = s_ref[after, todo] - mm(u_ref[done, after], u_ref[done, todo], 0, 0)
        y_next = r_ref[:, after] - mm(x_ref[:, done], u_ref[done, after], 1, 0)
        linv = block_inverse([dg_ref[8 * k : 8 * k + 8, :] for k in range(NB // 8)])
        linv_ref[...] = linv
        t_ref[oth, :, todo] = t_next
        for stage in range(len(stages) - 1, 0, -1):
            @pl.when(p >= stage)
            def _(stage=stage):
                advance(stage, p - stage)

        x_here = mm(y_ref[...], linv, 1, 1)
        x_ref[:, here] = x_here
        own_ref[p] = x_here.astype(jnp.bfloat16)
        keep(p).start()
        begin(0, p)
        u_after = mm(linv, t_ref[cur, :, after], 1, 0)
        dg_ref[...] = t_ref[oth, :, after] - mm(u_after, u_after, 0, 0)
        y_ref[...] = y_next - mm(x_here, u_after, 1, 0)
        return carry

    for at in range(0, steps, 2):
        lax.fori_loop(at, at + 2, functools.partial(step, begin_at=at, end_at=at + 2), 0)
    last = steps - 1
    for stage, p in [(4, last - 3), (3, last - 2), (2, last - 1), (1, last), (4, last - 2), (3, last - 1), (2, last), (4, last - 1), (3, last), (4, last)]:
        advance(stage, p)

    def end(p, carry):
        finish(len(stages) - 1, p)
        for stage in stages:
            for copy in stage(p):
                copy.wait_send()
        return carry

    lax.fori_loop(0, steps, end, 0)
    for i in range(half_steps):
        strip_sent(i).wait_send()


def factor(diag, rows, places):
    order = diag.shape[1]
    steps = order // NB
    per = rows.shape[0]
    nx, nz, ny = places
    sends = nz - 1 + nx - 1 + ny - 1 + 9
    vmem = pl.BlockSpec(memory_space=pltpu.VMEM)
    anywhere = pl.BlockSpec(memory_space=pl.ANY)
    dma = pltpu.SemaphoreType.DMA
    return pl.pallas_call(
        factor_kernel,
        out_shape=(
            jax.ShapeDtypeStruct(rows.shape, F32),
            jax.ShapeDtypeStruct((steps, 2, nx, nz, ny, per, NB), jnp.bfloat16),
        ),
        in_specs=[anywhere, vmem],
        out_specs=[vmem, anywhere],
        scratch_shapes=[
            pltpu.VMEM((order, order), F32),
            pltpu.VMEM((order, order), F32),
            pltpu.VMEM((2, NB, order), F32),
            pltpu.VMEM((NB, NB), F32),
            pltpu.VMEM((NB, NB), F32),
            pltpu.VMEM((per, NB), F32),
            pltpu.VMEM((steps, per, NB), jnp.bfloat16),
            dma((steps // 2,)),
            dma((steps,)),
            dma((steps, sends)),
            dma((steps, sends)),
            dma((steps,)),
        ],
        compiler_params=pltpu.CompilerParams(
            collective_id=0, has_side_effects=True, vmem_limit_bytes=60 << 20
        ),
    )(diag, rows)


def update_kernel(
    col_at, row_at, half, g_ref, blocks_ref, x_ref, out_ref, x_out,
    col_buf, row_buf, blk_buf, x_buf, col_sem, row_sem, blk_sem, x_sem,
):
    slots, stored, size, _ = blocks_ref.shape
    chunks = g_ref.shape[0]
    mine = half[0]

    def col_copy(s):
        return pltpu.make_async_copy(g_ref.at[:, :, jnp.maximum(col_at[s], 0)], col_buf.at[s], col_sem.at[s])

    def row_copy(s, r):
        at = jnp.maximum(row_at[s, r], 0)
        return pltpu.make_async_copy(g_ref.at[:, mine, at], row_buf.at[s, r], row_sem.at[s, r])

    def blk_in(s):
        return pltpu.make_async_copy(blocks_ref.at[s], blk_buf.at[s], blk_sem.at[s])

    def blk_out(s):
        return pltpu.make_async_copy(blk_buf.at[s], out_ref.at[s], blk_sem.at[s])

    x_in = pltpu.make_async_copy(x_ref, x_buf, x_sem.at[0])
    x_back = pltpu.make_async_copy(x_buf, x_out, x_sem.at[1])
    for s in range(slots):
        @pl.when(col_at[s] >= 0)
        def _():
            col_copy(s).start()
            for r in range(stored):
                row_copy(s, r).start()

    for s in range(slots):
        blk_in(s).start()
    x_in.start()

    for s in range(slots):
        @pl.when(col_at[s] < 0)
        def _():
            blk_in(s).wait()
            blk_out(s).start()

    x_in.wait()
    x_back.start()
    for s in range(slots):
        @pl.when(col_at[s] >= 0)
        def _():
            blk_in(s).wait()
            col_copy(s).wait()
            for r in range(stored):
                row_copy(s, r).wait()
            right = [
                jnp.concatenate([col_buf[s, p + q].reshape(2 * size, NB) for q in range(2)], axis=1)
                for p in range(0, chunks, 2)
            ]
            for r in range(stored):
                total = jnp.zeros((size, 2 * size), F32)
                for p in range(0, chunks, 2):
                    left = [row_buf[s, r, p + q].reshape(size, NB) for q in range(2)]
                    total += lax.dot_general(
                        jnp.concatenate(left, axis=1),
                        right[p // 2],
                        (((1,), (1,)), ((), ())),
                        preferred_element_type=F32,
                    )
                kept = blk_buf[s, r]
                blk_buf[s, r] = jnp.where(row_at[s, r] >= 0, kept - total, kept)
            blk_out(s).start()

    for s in range(slots):
        blk_out(s).wait()
    x_back.wait()


def update(g, blocks, x, col_at, row_at, half):
    slots, stored, size, width = blocks.shape
    chunks, _, _, parts, rows, _ = g.shape
    smem = pl.BlockSpec(memory_space=pltpu.SMEM)
    anywhere = pl.BlockSpec(memory_space=pl.ANY)
    return pl.pallas_call(
        update_kernel,
        out_shape=(jax.ShapeDtypeStruct(blocks.shape, F32), jax.ShapeDtypeStruct(x.shape, F32)),
        in_specs=[smem, smem, smem, anywhere, anywhere, anywhere],
        out_specs=[anywhere, anywhere],
        scratch_shapes=[
            pltpu.VMEM((slots, chunks, 2, parts, rows, NB), jnp.bfloat16),
            pltpu.VMEM((slots, stored, chunks, parts, rows, NB), jnp.bfloat16),
            pltpu.VMEM(blocks.shape, F32),
            pltpu.VMEM(x.shape, F32),
            pltpu.SemaphoreType.DMA((slots,)),
            pltpu.SemaphoreType.DMA((slots, stored)),
            pltpu.SemaphoreType.DMA((slots,)),
            pltpu.SemaphoreType.DMA((2,)),
        ],
        compiler_params=pltpu.CompilerParams(vmem_limit_bytes=60 << 20),
    )(col_at, row_at, half, g, blocks, x)


def places(ids, row_ids):
    match = row_ids == ids[..., None]
    at = jnp.arange(row_ids.shape[0], dtype=jnp.int32)
    return jnp.max(jnp.where(match, at, -1), axis=-1)


def local(diag_block, panel_rows, row_ids, col_ids, block_rows, blocks):
    pieces = row_ids.shape[0]
    col_at = places(col_ids, row_ids)
    row_at = places(block_rows, row_ids)
    half = lax.axis_index("row").astype(jnp.int32)[None]
    x, g = factor(diag_block, panel_rows[0], PLACES)
    g = g.reshape(g.shape[0], 2, pieces, -1, g.shape[5], NB)
    new_blocks, x = update(g, blocks, x, col_at, row_at, half)
    return x[None], new_blocks


def solution(mesh):
    return jax.shard_map(
        local,
        mesh=mesh,
        in_specs=(
            P("row", None),
            P("row", "blk", None),
            P(),
            P("blk"),
            P("blk", None),
            P("blk", None, "row", None),
        ),
        out_specs=(P("row", "blk", None), P("blk", None, "row", None)),
        check_vma=False,
    )
```

```python
import functools

import jax
import jax.numpy as jnp
from jax import lax
from jax.experimental import pallas as pl
from jax.experimental.pallas import tpu as pltpu
from jax.sharding import PartitionSpec as P

HIGH = lax.Precision.HIGHEST
NB = 128
F32 = jnp.float32
MESH = pl.DeviceIdType.MESH
LAGS = (0, 1, 2, 4, 5)
POINTS = ("outer", "inner", "outer", "inner", "outer")
PLACES = (4, 8, 4)


def lane_spread(x, c):
    return jnp.broadcast_to(x[:, c : c + 1], x.shape)


def row_spread(x, m):
    return jnp.broadcast_to(x[m : m + 1, :], x.shape)


def reciprocal(d):
    r = pl.reciprocal(d, approx=True)
    return r * (2.0 - d * r)


def mm(a, b, ca, cb):
    return lax.dot_general(
        a, b, (((ca,), (cb,)), ((), ())), precision=HIGH, preferred_element_type=F32
    )


def block_inverse(rows):
    sub = lax.broadcasted_iota(jnp.int32, (8, NB), 0)
    lane = lax.broadcasted_iota(jnp.int32, (8, NB), 1)
    n = NB // 8
    a = list(rows)
    e = [jnp.where(lane == sub + 8 * k, 1.0, 0.0).astype(F32) for k in range(n)]
    inverse = [None] * n
    pivot = [lane_spread(a[0], m) for m in range(8)]
    for j in range(n):
        d = list(pivot)
        unit = [jnp.where(sub == m, 1.0, 0.0).astype(F32) for m in range(8)]
        diagonal = jnp.ones((8, NB), F32)
        for i in range(8):
            top = row_spread(d[i], i)
            diagonal = jnp.where(sub == i, top, diagonal)
            if i == 7:
                break
            f = jnp.where(sub > i, d[i] * reciprocal(top), 0.0)
            for m in range(i + 1, 8):
                d[m] = d[m] - f * row_spread(d[i], m)
            for m in range(i + 1):
                unit[m] = unit[m] - f * row_spread(unit[m], i)
        scale = lax.rsqrt(diagonal)
        scale = scale * (1.5 - 0.5 * diagonal * scale * scale)
        w = [unit[m] * scale for m in range(8)]
        u = w[0] * row_spread(a[j], 0)
        v = w[0] * row_spread(e[j], 0)
        for m in range(1, 8):
            u = u + w[m] * row_spread(a[j], m)
            v = v + w[m] * row_spread(e[j], m)
        inverse[j] = v
        if j == n - 1:
            break
        ws = {(i, m): row_spread(w[m], i) for i in range(8) for m in range(i + 1)}
        us = [row_spread(u, i) for i in range(8)]
        vs = [row_spread(v, i) for i in range(8)]
        for k in range(j + 1, n):
            below = [lane_spread(a[k], 8 * j + m) for m in range(8)]
            c = []
            for i in range(8):
                t = below[0] * ws[i, 0]
                for m in range(1, i + 1):
                    t = t + below[m] * ws[i, m]
                c.append(t)
            if k == j + 1:
                pivot = []
                for m in range(8):
                    t = c[0] * row_spread(c[0], m)
                    for i in range(1, 8):
                        t = t + c[i] * row_spread(c[i], m)
                    pivot.append(lane_spread(a[k], 8 * k + m) - t)
            ta, te = c[0] * us[0], c[0] * vs[0]
            for i in range(1, 8):
                ta = ta + c[i] * us[i]
                te = te + c[i] * vs[i]
            a[k] = a[k] - ta
            e[k] = e[k] - te
    return jnp.concatenate(inverse, axis=0)


def spreading(g_ref, own_ref, send_sem, recv_sem, local_sem):
    _, _, nx, nz, ny, rows, _ = g_ref.shape
    blk, h = lax.axis_index("blk"), lax.axis_index("row")
    x, z, y = blk // (nz * ny), (blk // ny) % nz, blk % ny
    first, second = pl.ds(0, rows // 2), pl.ds(rows // 2, rows // 2)
    every = slice(None)

    def device(x, z, y, h):
        return ((x * nz + z) * ny + y, h)

    along_x = [device((x + k) % nx, z, y, h) for k in range(1, nx)]
    along_z = [device(x, (z + k) % nz, y, h) for k in range(1, nz)]
    along_y = [device(x, z, (y + k) % ny, h) for k in range(1, ny)]
    other = device(x, z, y, 1 - h)

    def copies(p, at, pieces):
        return [
            pltpu.make_async_remote_copy(
                src_ref=src,
                dst_ref=dst,
                send_sem=send_sem.at[p, at + i],
                recv_sem=recv_sem.at[p, at + i],
                device_id=target,
                device_id_type=MESH,
            )
            for i, (src, dst, target) in enumerate(pieces)
        ]

    def to_z(p):
        return copies(p, 0, [(own_ref.at[p], g_ref.at[p, h, x, z, y], d) for d in along_z])

    def to_plane(p):
        a, b = g_ref.at[p, h, x, every, y, first], g_ref.at[p, h, x, every, y, second]
        return copies(p, nz - 1, [(a, a, d) for d in along_y] + [(b, b, d) for d in along_x])

    plane = nz - 1 + nx - 1 + ny - 1
    right, left = (x + 1) % nx, (x + nx - 1) % nx
    up, down = (y + 1) % ny, (y + ny - 1) % ny

    def to_next(p):
        a, b = g_ref.at[p, h, x, every, every, first], g_ref.at[p, h, every, every, y, second]
        return copies(p, plane, [
            (a, a, device(right, z, y, h)), (a, a, device(left, z, y, h)),
            (b, b, device(x, z, up, h)), (b, b, device(x, z, down, h)),
        ])

    def to_far(p):
        low, high = pl.ds(0, nz // 2), pl.ds(nz // 2, nz // 2)
        a, b = g_ref.at[p, h, left, low, every, first], g_ref.at[p, h, right, high, every, first]
        c, d = g_ref.at[p, h, every, low, down, second], g_ref.at[p, h, every, high, up, second]
        return copies(p, plane + 4, [
            (a, a, device(right, z, y, h)), (b, b, device(left, z, y, h)),
            (c, c, device(x, z, up, h)), (d, d, device(x, z, down, h)),
        ])

    def to_core(p):
        return copies(p, plane + 8, [(g_ref.at[p, h], g_ref.at[p, h], other)])

    def keep(p):
        return pltpu.make_async_copy(own_ref.at[p], g_ref.at[p, h, x, z, y], local_sem.at[p])

    return [to_z, to_plane, to_next, to_far, to_core], keep, along_x + along_z + along_y + [other]


def factor_kernel(
    row_ids, col_ids, block_rows, diag_ref, r_ref, x_ref, g_ref, col_at, row_at,
    s_ref, u_ref, t_ref, linv_ref, dg_ref, y_ref, own_ref,
    strip_send, strip_sem, send_sem, recv_sem, local_sem,
):
    steps = s_ref.shape[0] // NB
    half_steps = steps // 2
    blk, h = lax.axis_index("blk"), lax.axis_index("row")
    stages, keep, peers = spreading(g_ref, own_ref, send_sem, recv_sem, local_sem)

    def strip(i):
        return diag_ref.at[pl.ds(i * NB, NB)], s_ref.at[pl.ds(pl.multiple_of((half_steps * h + i) * NB, NB), NB)]

    def strip_copy(i):
        src, dst = strip(i)
        return pltpu.make_async_copy(src, dst, strip_sem.at[half_steps * h + i])

    def strip_sent(i):
        src, dst = strip(i)
        return pltpu.make_async_remote_copy(
            src_ref=src,
            dst_ref=dst,
            send_sem=strip_send.at[i],
            recv_sem=strip_sem.at[half_steps * h + i],
            device_id=(blk, 1 - h),
            device_id_type=MESH,
        )

    def strip_wait(q):
        dst = s_ref.at[pl.ds(pl.multiple_of(q * NB, NB), NB)]
        pltpu.make_async_copy(diag_ref.at[pl.ds(0, NB)], dst, strip_sem.at[q]).wait()

    def finish(stage, p):
        for copy in stages[stage](p):
            copy.wait_recv()

    def begin(stage, p):
        for copy in stages[stage](p):
            copy.start()

    def advance(stage, p):
        finish(stage - 1, p)
        if stage == 1:
            keep(p).wait()
        begin(stage, p)

    for i in range(half_steps):
        strip_copy(i).start()
    barrier = pltpu.get_barrier_semaphore()
    for peer in peers:
        pl.semaphore_signal(barrier, inc=1, device_id=peer, device_id_type=MESH)
    u_ref[...] = jnp.zeros_like(u_ref)
    x_ref[...] = jnp.zeros_like(x_ref)
    linv_ref[...] = jnp.zeros_like(linv_ref)
    t_ref[1] = jnp.zeros(t_ref.shape[1:], F32)
    y_ref[...] = r_ref[:, 0:NB]
    for ids, at in ((col_ids, col_at), (block_rows, row_at)):
        found = jnp.full(ids.shape, -1, jnp.int32)
        for k in range(row_ids.shape[0]):
            found = jnp.where(ids[...] == row_ids[k], k, found)
        at[...] = found
    pl.semaphore_wait(barrier, len(peers))
    for i in range(half_steps):
        strip_sent(i).start()
    strip_wait(0)
    t_ref[0] = s_ref[0:NB, :]
    dg_ref[...] = s_ref[0:NB, 0:NB]

    def step(p, carry, begin_at, end_at):
        @pl.when(p + 1 < steps)
        def _():
            strip_wait(p + 1)

        cur = lax.rem(p, 2)
        oth = 1 - cur
        done, todo = slice(0, (end_at - 1) * NB), slice(begin_at * NB, steps * NB)
        here = pl.ds(pl.multiple_of(p * NB, NB), NB)
        before = pl.ds(pl.multiple_of(jnp.maximum(p - 1, 0) * NB, NB), NB)
        after = pl.ds(pl.multiple_of(jnp.minimum(p + 1, steps - 1) * NB, NB), NB)
        u_prev = mm(linv_ref[...], t_ref[oth, :, todo], 1, 0)
        u_ref[before, todo] = u_prev
        t_ref[cur, :, todo] = t_ref[cur, :, todo] - mm(u_ref[before, here], u_prev, 0, 0)
        t_next = s_ref[after, todo] - mm(u_ref[done, after], u_ref[done, todo], 0, 0)
        y_next = r_ref[:, after] - mm(x_ref[:, done], u_ref[done, after], 1, 0)
        linv = block_inverse([dg_ref[8 * k : 8 * k + 8, :] for k in range(NB // 8)])
        linv_ref[...] = linv
        t_ref[oth, :, todo] = t_next

        def advance_due(point):
            for stage in range(len(stages) - 1, 0, -1):
                if POINTS[stage] == point:
                    @pl.when(p >= LAGS[stage])
                    def _(stage=stage):
                        advance(stage, p - LAGS[stage])

        advance_due("inner")
        x_here = mm(y_ref[...], linv, 1, 1)
        x_ref[:, here] = x_here
        own_ref[p] = x_here.astype(jnp.bfloat16)
        keep(p).start()
        begin(0, p)
        u_after = mm(linv, t_ref[cur, :, after], 1, 0)
        dg_ref[...] = t_ref[oth, :, after] - mm(u_after, u_after, 0, 0)
        y_ref[...] = y_next - mm(x_here, u_after, 1, 0)
        advance_due("outer")
        return carry

    for at in range(0, steps, 2):
        lax.fori_loop(at, at + 2, functools.partial(step, begin_at=at, end_at=at + 2), 0)
    left = [(p + stage, -stage) for stage in range(1, len(stages)) for p in range(steps) if p + LAGS[stage] >= steps]
    for when, stage in sorted(left):
        advance(-stage, when + stage)

    def end(p, carry):
        finish(len(stages) - 1, p)
        for stage in stages:
            for copy in stage(p):
                copy.wait_send()
        return carry

    lax.fori_loop(0, steps, end, 0)
    for i in range(half_steps):
        strip_sent(i).wait_send()


def factor(row_ids, col_ids, block_rows, diag, rows, places):
    order = diag.shape[1]
    steps = order // NB
    per = rows.shape[0]
    nx, nz, ny = places
    sends = nz - 1 + nx - 1 + ny - 1 + 9
    vmem = pl.BlockSpec(memory_space=pltpu.VMEM)
    anywhere = pl.BlockSpec(memory_space=pl.ANY)
    dma = pltpu.SemaphoreType.DMA
    return pl.pallas_call(
        factor_kernel,
        out_shape=(
            jax.ShapeDtypeStruct(rows.shape, F32),
            jax.ShapeDtypeStruct((steps, 2, nx, nz, ny, per, NB), jnp.bfloat16),
            jax.ShapeDtypeStruct(col_ids.shape, jnp.int32),
            jax.ShapeDtypeStruct(block_rows.shape, jnp.int32),
        ),
        in_specs=[pl.BlockSpec(memory_space=pltpu.SMEM), vmem, vmem, anywhere, vmem],
        out_specs=[vmem, anywhere, vmem, vmem],
        scratch_shapes=[
            pltpu.VMEM((order, order), F32),
            pltpu.VMEM((order, order), F32),
            pltpu.VMEM((2, NB, order), F32),
            pltpu.VMEM((NB, NB), F32),
            pltpu.VMEM((NB, NB), F32),
            pltpu.VMEM((per, NB), F32),
            pltpu.VMEM((steps, per, NB), jnp.bfloat16),
            dma((steps // 2,)),
            dma((steps,)),
            dma((steps, sends)),
            dma((steps, sends)),
            dma((steps,)),
        ],
        compiler_params=pltpu.CompilerParams(
            collective_id=0, has_side_effects=True, vmem_limit_bytes=60 << 20
        ),
    )(row_ids, col_ids, block_rows, diag, rows)


def update_kernel(
    col_at, row_at, half, g_ref, blocks_ref, x_ref, out_ref, x_out,
    col_buf, row_buf, blk_buf, x_buf, col_sem, row_sem, blk_sem, x_sem,
):
    slots, stored, size, _ = blocks_ref.shape
    chunks = g_ref.shape[0]
    mine = half[0]

    def col_copy(s):
        return pltpu.make_async_copy(g_ref.at[:, :, jnp.maximum(col_at[0, s], 0)], col_buf.at[s], col_sem.at[s])

    def row_copy(s, r):
        at = jnp.maximum(row_at[s, r], 0)
        return pltpu.make_async_copy(g_ref.at[:, mine, at], row_buf.at[s, r], row_sem.at[s, r])

    def blk_in(s):
        return pltpu.make_async_copy(blocks_ref.at[s], blk_buf.at[s], blk_sem.at[s])

    def blk_out(s):
        return pltpu.make_async_copy(blk_buf.at[s], out_ref.at[s], blk_sem.at[s])

    x_in = pltpu.make_async_copy(x_ref, x_buf, x_sem.at[0])
    x_back = pltpu.make_async_copy(x_buf, x_out, x_sem.at[1])
    for s in range(slots):
        @pl.when(col_at[0, s] >= 0)
        def _():
            col_copy(s).start()
            for r in range(stored):
                row_copy(s, r).start()

    for s in range(slots):
        blk_in(s).start()
    x_in.start()

    for s in range(slots):
        @pl.when(col_at[0, s] < 0)
        def _():
            blk_in(s).wait()
            blk_out(s).start()

    x_in.wait()
    x_back.start()
    for s in range(slots):
        @pl.when(col_at[0, s] >= 0)
        def _():
            blk_in(s).wait()
            col_copy(s).wait()
            for r in range(stored):
                row_copy(s, r).wait()
            right = [
                jnp.concatenate([col_buf[s, p + q].reshape(2 * size, NB) for q in range(2)], axis=1)
                for p in range(0, chunks, 2)
            ]
            for r in range(stored):
                total = jnp.zeros((size, 2 * size), F32)
                for p in range(0, chunks, 2):
                    left = [row_buf[s, r, p + q].reshape(size, NB) for q in range(2)]
                    total += lax.dot_general(
                        jnp.concatenate(left, axis=1),
                        right[p // 2],
                        (((1,), (1,)), ((), ())),
                        preferred_element_type=F32,
                    )
                kept = blk_buf[s, r]
                blk_buf[s, r] = jnp.where(row_at[s, r] >= 0, kept - total, kept)
            blk_out(s).start()

    for s in range(slots):
        blk_out(s).wait()
    x_back.wait()


def update(g, blocks, x, col_at, row_at, half):
    slots, stored, size, width = blocks.shape
    chunks, _, _, parts, rows, _ = g.shape
    smem = pl.BlockSpec(memory_space=pltpu.SMEM)
    anywhere = pl.BlockSpec(memory_space=pl.ANY)
    return pl.pallas_call(
        update_kernel,
        out_shape=(jax.ShapeDtypeStruct(blocks.shape, F32), jax.ShapeDtypeStruct(x.shape, F32)),
        in_specs=[smem, smem, smem, anywhere, anywhere, anywhere],
        out_specs=[anywhere, anywhere],
        scratch_shapes=[
            pltpu.VMEM((slots, chunks, 2, parts, rows, NB), jnp.bfloat16),
            pltpu.VMEM((slots, stored, chunks, parts, rows, NB), jnp.bfloat16),
            pltpu.VMEM(blocks.shape, F32),
            pltpu.VMEM(x.shape, F32),
            pltpu.SemaphoreType.DMA((slots,)),
            pltpu.SemaphoreType.DMA((slots, stored)),
            pltpu.SemaphoreType.DMA((slots,)),
            pltpu.SemaphoreType.DMA((2,)),
        ],
        compiler_params=pltpu.CompilerParams(vmem_limit_bytes=60 << 20),
    )(col_at, row_at, half, g, blocks, x)


def local(diag_block, panel_rows, row_ids, col_ids, block_rows, blocks):
    pieces = row_ids.shape[0]
    half = lax.axis_index("row").astype(jnp.int32)[None]
    x, g, col_at, row_at = factor(row_ids, col_ids[None], block_rows, diag_block, panel_rows[0], PLACES)
    g = g.reshape(g.shape[0], 2, pieces, -1, g.shape[5], NB)
    new_blocks, x = update(g, blocks, x, col_at, row_at, half)
    return x[None], new_blocks


def solution(mesh):
    return jax.shard_map(
        local,
        mesh=mesh,
        in_specs=(
            P("row", None),
            P("row", "blk", None),
            P(),
            P("blk"),
            P("blk", None),
            P("blk", None, "row", None),
        ),
        out_specs=(P("row", "blk", None), P("blk", None, "row", None)),
        check_vma=False,
    )
```

```python
import functools

import jax
import jax.numpy as jnp
from jax import lax
from jax.experimental import pallas as pl
from jax.experimental.pallas import tpu as pltpu
from jax.sharding import PartitionSpec as P

HIGH = lax.Precision.HIGHEST
NB = 128
F32 = jnp.float32
MESH = pl.DeviceIdType.MESH
LAGS = (0, 1, 2, 4, 5)
POINTS = ("outer", "inner", "outer", "inner", "outer")
PLACES = (4, 8, 4)


def lane_spread(x, c):
    return jnp.broadcast_to(x[:, c : c + 1], x.shape)


def row_spread(x, m):
    return jnp.broadcast_to(x[m : m + 1, :], x.shape)


def reciprocal(d):
    r = pl.reciprocal(d, approx=True)
    return r * (2.0 - d * r)


def mm(a, b, ca, cb):
    return lax.dot_general(
        a, b, (((ca,), (cb,)), ((), ())), precision=HIGH, preferred_element_type=F32
    )


def block_inverse(rows):
    sub = lax.broadcasted_iota(jnp.int32, (8, NB), 0)
    lane = lax.broadcasted_iota(jnp.int32, (8, NB), 1)
    n = NB // 8
    a = list(rows)
    e = [jnp.where(lane == sub + 8 * k, 1.0, 0.0).astype(F32) for k in range(n)]
    inverse = [None] * n
    pivot = [lane_spread(a[0], m) for m in range(8)]
    for j in range(n):
        d = list(pivot)
        unit = [jnp.where(sub == m, 1.0, 0.0).astype(F32) for m in range(8)]
        diagonal = jnp.ones((8, NB), F32)
        for i in range(8):
            top = row_spread(d[i], i)
            diagonal = jnp.where(sub == i, top, diagonal)
            if i == 7:
                break
            f = jnp.where(sub > i, d[i] * reciprocal(top), 0.0)
            for m in range(i + 1, 8):
                d[m] = d[m] - f * row_spread(d[i], m)
            for m in range(i + 1):
                unit[m] = unit[m] - f * row_spread(unit[m], i)
        scale = lax.rsqrt(diagonal)
        scale = scale * (1.5 - 0.5 * diagonal * scale * scale)
        w = [unit[m] * scale for m in range(8)]
        u = w[0] * row_spread(a[j], 0)
        v = w[0] * row_spread(e[j], 0)
        for m in range(1, 8):
            u = u + w[m] * row_spread(a[j], m)
            v = v + w[m] * row_spread(e[j], m)
        inverse[j] = v
        if j == n - 1:
            break
        ws = {(i, m): row_spread(w[m], i) for i in range(8) for m in range(i + 1)}
        us = [row_spread(u, i) for i in range(8)]
        vs = [row_spread(v, i) for i in range(8)]
        for k in range(j + 1, n):
            below = [lane_spread(a[k], 8 * j + m) for m in range(8)]
            c = []
            for i in range(8):
                t = below[0] * ws[i, 0]
                for m in range(1, i + 1):
                    t = t + below[m] * ws[i, m]
                c.append(t)
            if k == j + 1:
                pivot = []
                for m in range(8):
                    t = c[0] * row_spread(c[0], m)
                    for i in range(1, 8):
                        t = t + c[i] * row_spread(c[i], m)
                    pivot.append(lane_spread(a[k], 8 * k + m) - t)
            ta, te = c[0] * us[0], c[0] * vs[0]
            for i in range(1, 8):
                ta = ta + c[i] * us[i]
                te = te + c[i] * vs[i]
            a[k] = a[k] - ta
            e[k] = e[k] - te
    return jnp.concatenate(inverse, axis=0)


def spreading(g_ref, own_ref, send_sem, recv_sem, local_sem):
    _, _, nx, nz, ny, rows, _ = g_ref.shape
    blk, h = lax.axis_index("blk"), lax.axis_index("row")
    x, z, y = blk // (nz * ny), (blk // ny) % nz, blk % ny
    first, second = pl.ds(0, rows // 2), pl.ds(rows // 2, rows // 2)
    every = slice(None)

    def device(x, z, y, h):
        return ((x * nz + z) * ny + y, h)

    along_x = [device((x + k) % nx, z, y, h) for k in range(1, nx)]
    along_z = [device(x, (z + k) % nz, y, h) for k in range(1, nz)]
    along_y = [device(x, z, (y + k) % ny, h) for k in range(1, ny)]
    other = device(x, z, y, 1 - h)

    def copies(p, at, pieces):
        return [
            pltpu.make_async_remote_copy(
                src_ref=src,
                dst_ref=dst,
                send_sem=send_sem.at[p, at + i],
                recv_sem=recv_sem.at[p, at + i],
                device_id=target,
                device_id_type=MESH,
            )
            for i, (src, dst, target) in enumerate(pieces)
        ]

    def to_z(p):
        return copies(p, 0, [(own_ref.at[p], g_ref.at[p, h, x, z, y], d) for d in along_z])

    def to_plane(p):
        a, b = g_ref.at[p, h, x, every, y, first], g_ref.at[p, h, x, every, y, second]
        return copies(p, nz - 1, [(a, a, d) for d in along_y] + [(b, b, d) for d in along_x])

    plane = nz - 1 + nx - 1 + ny - 1
    right, left = (x + 1) % nx, (x + nx - 1) % nx
    up, down = (y + 1) % ny, (y + ny - 1) % ny

    def to_next(p):
        a, b = g_ref.at[p, h, x, every, every, first], g_ref.at[p, h, every, every, y, second]
        return copies(p, plane, [
            (a, a, device(right, z, y, h)), (a, a, device(left, z, y, h)),
            (b, b, device(x, z, up, h)), (b, b, device(x, z, down, h)),
        ])

    def to_far(p):
        low, high = pl.ds(0, nz // 2), pl.ds(nz // 2, nz // 2)
        a, b = g_ref.at[p, h, left, low, every, first], g_ref.at[p, h, right, high, every, first]
        c, d = g_ref.at[p, h, every, low, down, second], g_ref.at[p, h, every, high, up, second]
        return copies(p, plane + 4, [
            (a, a, device(right, z, y, h)), (b, b, device(left, z, y, h)),
            (c, c, device(x, z, up, h)), (d, d, device(x, z, down, h)),
        ])

    def to_core(p):
        return copies(p, plane + 8, [(g_ref.at[p, h], g_ref.at[p, h], other)])

    def keep(p):
        return pltpu.make_async_copy(own_ref.at[p], g_ref.at[p, h, x, z, y], local_sem.at[p])

    return [to_z, to_plane, to_next, to_far, to_core], keep, along_x + along_z + along_y + [other]


def factor_kernel(
    row_ids, col_ids, block_rows, diag_ref, r_ref, x_ref, g_ref, col_at, row_at,
    s_ref, u_ref, t_ref, linv_ref, dg_ref, y_ref, own_ref,
    strip_send, strip_sem, send_sem, recv_sem, local_sem,
):
    steps = s_ref.shape[0] // NB
    half_steps = steps // 2
    blk, h = lax.axis_index("blk"), lax.axis_index("row")
    stages, keep, peers = spreading(g_ref, own_ref, send_sem, recv_sem, local_sem)

    def strip(i):
        return diag_ref.at[pl.ds(i * NB, NB)], s_ref.at[pl.ds(pl.multiple_of((half_steps * h + i) * NB, NB), NB)]

    def strip_copy(i):
        src, dst = strip(i)
        return pltpu.make_async_copy(src, dst, strip_sem.at[half_steps * h + i])

    def strip_sent(i):
        src, dst = strip(i)
        return pltpu.make_async_remote_copy(
            src_ref=src,
            dst_ref=dst,
            send_sem=strip_send.at[i],
            recv_sem=strip_sem.at[half_steps * h + i],
            device_id=(blk, 1 - h),
            device_id_type=MESH,
        )

    def strip_wait(q):
        dst = s_ref.at[pl.ds(pl.multiple_of(q * NB, NB), NB)]
        pltpu.make_async_copy(diag_ref.at[pl.ds(0, NB)], dst, strip_sem.at[q]).wait()

    def finish(stage, p):
        for copy in stages[stage](p):
            copy.wait_recv()

    def begin(stage, p):
        for copy in stages[stage](p):
            copy.start()

    def advance(stage, p):
        finish(stage - 1, p)
        if stage == 1:
            keep(p).wait()
        begin(stage, p)

    for i in range(half_steps):
        strip_copy(i).start()
    barrier = pltpu.get_barrier_semaphore()
    for peer in peers:
        pl.semaphore_signal(barrier, inc=1, device_id=peer, device_id_type=MESH)
    u_ref[...] = jnp.zeros_like(u_ref)
    x_ref[...] = jnp.zeros_like(x_ref)
    linv_ref[...] = jnp.zeros_like(linv_ref)
    t_ref[1] = jnp.zeros(t_ref.shape[1:], F32)
    y_ref[...] = r_ref[:, 0:NB]
    for ids, at in ((col_ids, col_at), (block_rows, row_at)):
        found = jnp.full(ids.shape, -1, jnp.int32)
        for k in range(row_ids.shape[0]):
            found = jnp.where(ids[...] == row_ids[k], k, found)
        at[...] = found
    pl.semaphore_wait(barrier, len(peers))
    for i in range(half_steps):
        strip_sent(i).start()
    strip_wait(0)
    t_ref[0] = s_ref[0:NB, :]
    dg_ref[...] = s_ref[0:NB, 0:NB]

    def step(p, carry, begin_at, end_at):
        @pl.when(p + 1 < steps)
        def _():
            strip_wait(p + 1)

        cur = lax.rem(p, 2)
        oth = 1 - cur
        done, todo = slice(0, (end_at - 1) * NB), slice(begin_at * NB, steps * NB)
        here = pl.ds(pl.multiple_of(p * NB, NB), NB)
        before = pl.ds(pl.multiple_of(jnp.maximum(p - 1, 0) * NB, NB), NB)
        after = pl.ds(pl.multiple_of(jnp.minimum(p + 1, steps - 1) * NB, NB), NB)
        u_prev = mm(linv_ref[...], t_ref[oth, :, todo], 1, 0)
        u_ref[before, todo] = u_prev
        t_ref[cur, :, todo] = t_ref[cur, :, todo] - mm(u_ref[before, here], u_prev, 0, 0)
        t_next = s_ref[after, todo] - mm(u_ref[done, after], u_ref[done, todo], 0, 0)
        y_next = r_ref[:, after] - mm(x_ref[:, done], u_ref[done, after], 1, 0)
        linv = block_inverse([dg_ref[8 * k : 8 * k + 8, :] for k in range(NB // 8)])
        linv_ref[...] = linv
        t_ref[oth, :, todo] = t_next

        def advance_due(point):
            for stage in range(len(stages) - 1, 0, -1):
                if POINTS[stage] == point:
                    @pl.when(p >= LAGS[stage])
                    def _(stage=stage):
                        advance(stage, p - LAGS[stage])

        advance_due("inner")
        x_here = mm(y_ref[...], linv, 1, 1)
        x_ref[:, here] = x_here
        own_ref[p] = x_here.astype(jnp.bfloat16)
        keep(p).start()
        begin(0, p)
        u_after = mm(linv, t_ref[cur, :, after], 1, 0)
        dg_ref[...] = t_ref[oth, :, after] - mm(u_after, u_after, 0, 0)
        y_ref[...] = y_next - mm(x_here, u_after, 1, 0)
        advance_due("outer")
        return carry

    for at in range(0, steps, 2):
        lax.fori_loop(at, at + 2, functools.partial(step, begin_at=at, end_at=at + 2), 0)
    left = [(stage, p) for stage in range(1, len(stages)) for p in range(steps) if p + LAGS[stage] >= steps]
    for stage, p in sorted(left, key=lambda due: (due[1] + 2 * due[0], -due[0])):
        advance(stage, p)

    def end(p, carry):
        finish(len(stages) - 1, p)
        for stage in stages:
            for copy in stage(p):
                copy.wait_send()
        return carry

    lax.fori_loop(0, steps, end, 0)
    for i in range(half_steps):
        strip_sent(i).wait_send()


def factor(row_ids, col_ids, block_rows, diag, rows, places):
    order = diag.shape[1]
    steps = order // NB
    per = rows.shape[0]
    nx, nz, ny = places
    sends = nz - 1 + nx - 1 + ny - 1 + 9
    vmem = pl.BlockSpec(memory_space=pltpu.VMEM)
    anywhere = pl.BlockSpec(memory_space=pl.ANY)
    dma = pltpu.SemaphoreType.DMA
    return pl.pallas_call(
        factor_kernel,
        out_shape=(
            jax.ShapeDtypeStruct(rows.shape, F32),
            jax.ShapeDtypeStruct((steps, 2, nx, nz, ny, per, NB), jnp.bfloat16),
            jax.ShapeDtypeStruct(col_ids.shape, jnp.int32),
            jax.ShapeDtypeStruct(block_rows.shape, jnp.int32),
        ),
        in_specs=[pl.BlockSpec(memory_space=pltpu.SMEM), vmem, vmem, anywhere, vmem],
        out_specs=[vmem, anywhere, vmem, vmem],
        scratch_shapes=[
            pltpu.VMEM((order, order), F32),
            pltpu.VMEM((order, order), F32),
            pltpu.VMEM((2, NB, order), F32),
            pltpu.VMEM((NB, NB), F32),
            pltpu.VMEM((NB, NB), F32),
            pltpu.VMEM((per, NB), F32),
            pltpu.VMEM((steps, per, NB), jnp.bfloat16),
            dma((steps // 2,)),
            dma((steps,)),
            dma((steps, sends)),
            dma((steps, sends)),
            dma((steps,)),
        ],
        compiler_params=pltpu.CompilerParams(
            collective_id=0, has_side_effects=True, vmem_limit_bytes=60 << 20
        ),
    )(row_ids, col_ids, block_rows, diag, rows)


def update_kernel(
    col_at, row_at, half, g_ref, blocks_ref, x_ref, out_ref, x_out,
    col_buf, row_buf, blk_buf, x_buf, col_sem, row_sem, blk_sem, x_sem,
):
    slots, stored, size, _ = blocks_ref.shape
    chunks = g_ref.shape[0]
    mine = half[0]

    def col_copy(s):
        return pltpu.make_async_copy(g_ref.at[:, :, jnp.maximum(col_at[0, s], 0)], col_buf.at[s], col_sem.at[s])

    def row_copy(s, r):
        at = jnp.maximum(row_at[s, r], 0)
        return pltpu.make_async_copy(g_ref.at[:, mine, at], row_buf.at[s, r], row_sem.at[s, r])

    def blk_in(s):
        return pltpu.make_async_copy(blocks_ref.at[s], blk_buf.at[s], blk_sem.at[s])

    def blk_out(s):
        return pltpu.make_async_copy(blk_buf.at[s], out_ref.at[s], blk_sem.at[s])

    x_in = pltpu.make_async_copy(x_ref, x_buf, x_sem.at[0])
    x_back = pltpu.make_async_copy(x_buf, x_out, x_sem.at[1])
    x_in.start()
    for s in range(slots):
        @pl.when(col_at[0, s] >= 0)
        def _():
            col_copy(s).start()
            for r in range(stored):
                row_copy(s, r).start()
            blk_in(s).start()

    for s in range(slots):
        @pl.when(col_at[0, s] < 0)
        def _():
            blk_in(s).start()

    x_in.wait()
    x_back.start()
    for s in range(slots):
        @pl.when(col_at[0, s] >= 0)
        def _():
            blk_in(s).wait()
            col_copy(s).wait()
            for r in range(stored):
                row_copy(s, r).wait()
            right = [
                jnp.concatenate([col_buf[s, p + q].reshape(2 * size, NB) for q in range(2)], axis=1)
                for p in range(0, chunks, 2)
            ]
            for r in range(stored):
                total = jnp.zeros((size, 2 * size), F32)
                for p in range(0, chunks, 2):
                    left = [row_buf[s, r, p + q].reshape(size, NB) for q in range(2)]
                    total += lax.dot_general(
                        jnp.concatenate(left, axis=1),
                        right[p // 2],
                        (((1,), (1,)), ((), ())),
                        preferred_element_type=F32,
                    )
                kept = blk_buf[s, r]
                blk_buf[s, r] = jnp.where(row_at[s, r] >= 0, kept - total, kept)
            blk_out(s).start()

    for s in range(slots):
        @pl.when(col_at[0, s] < 0)
        def _():
            blk_in(s).wait()
            blk_out(s).start()

    for s in range(slots):
        blk_out(s).wait()
    x_back.wait()


def update(g, blocks, x, col_at, row_at, half):
    slots, stored, size, width = blocks.shape
    chunks, _, _, parts, rows, _ = g.shape
    smem = pl.BlockSpec(memory_space=pltpu.SMEM)
    anywhere = pl.BlockSpec(memory_space=pl.ANY)
    return pl.pallas_call(
        update_kernel,
        out_shape=(jax.ShapeDtypeStruct(blocks.shape, F32), jax.ShapeDtypeStruct(x.shape, F32)),
        in_specs=[smem, smem, smem, anywhere, anywhere, anywhere],
        out_specs=[anywhere, anywhere],
        scratch_shapes=[
            pltpu.VMEM((slots, chunks, 2, parts, rows, NB), jnp.bfloat16),
            pltpu.VMEM((slots, stored, chunks, parts, rows, NB), jnp.bfloat16),
            pltpu.VMEM(blocks.shape, F32),
            pltpu.VMEM(x.shape, F32),
            pltpu.SemaphoreType.DMA((slots,)),
            pltpu.SemaphoreType.DMA((slots, stored)),
            pltpu.SemaphoreType.DMA((slots,)),
            pltpu.SemaphoreType.DMA((2,)),
        ],
        compiler_params=pltpu.CompilerParams(vmem_limit_bytes=60 << 20),
    )(col_at, row_at, half, g, blocks, x)


def local(diag_block, panel_rows, row_ids, col_ids, block_rows, blocks):
    pieces = row_ids.shape[0]
    half = lax.axis_index("row").astype(jnp.int32)[None]
    x, g, col_at, row_at = factor(row_ids, col_ids[None], block_rows, diag_block, panel_rows[0], PLACES)
    g = g.reshape(g.shape[0], 2, pieces, -1, g.shape[5], NB)
    new_blocks, x = update(g, blocks, x, col_at, row_at, half)
    return x[None], new_blocks


def solution(mesh):
    return jax.shard_map(
        local,
        mesh=mesh,
        in_specs=(
            P("row", None),
            P("row", "blk", None),
            P(),
            P("blk"),
            P("blk", None),
            P("blk", None, "row", None),
        ),
        out_specs=(P("row", "blk", None), P("blk", None, "row", None)),
        check_vma=False,
    )
```
